32 devices in a mesh: dp: 2 (over y), expert: 16 (over z, x, core).
Axes of the slice: x: 2, y: 2, z: 4, core: 2. Of those that a mesh axis runs over, the one named last changes fastest.
Arguments:
- grad_out: bfloat16 [4096, 4096], P(('dp', 'expert')), may hold values from -6 to 6
- saved_pre: bfloat16 [4096, 2, 1536], P(('dp', 'expert')), may hold values from -6 to 6
- gate_weight: bfloat16 [4096, 2], P(('dp', 'expert')), may hold values from 0.049804688 to 0.59765625
- routes: int32 [4096, 2], P(('dp', 'expert')), may hold values from 0 to 15, all different within a row; in each aligned block of 128 rows (0 to 127, 128 to 255, ...) at most 20 rows name the same one
- w_down: bfloat16 [16, 768, 4096], P('expert', None, 'dp'), may hold values from -0.09375 to 0.09375
Outputs:
- grad_pre: bfloat16 [4096, 2, 1536], P(('dp', 'expert'))
- grad_gate: bfloat16 [4096, 2], P(('dp', 'expert'))
- grad_down: bfloat16 [16, 768, 4096], P('expert', None, 'dp')
The draws below stay inside these ranges and needn't reach their ends.
Inputs may be any that keep to these rules, and one draw needn't show every extreme that they name: Among the routes of one device's 128 tokens no expert is named more than 20 times, a bound that some block reaches; a token names 2 different experts.
All inputs are finite; a program needn't handle non-finite values.
Results may differ from the reference program's by a relative error of at most 0.0085.
Values may be sent and summed in bfloat16 or wider, within the bound.
A program may use at most 128 MiB of HBM per device.

```python
import math
import jax
import jax.numpy as jnp
import numpy as np
from jax import lax

D = 4096
HID = 768
TOP = 2
TOK_DEV = 128
EXPERTS = 16
CAP = 20
TOKENS = 4096
N_DP = 2
N_EXPERT = 16


def shard_levels(key, dims, split, low, high):
    level, own = 1.0, jax.random.fold_in(key, 6)
    for axis_at, shards_of in split:
        heights = jnp.exp(jax.random.uniform(jax.random.fold_in(own, axis_at), (shards_of,), jnp.float32, low / len(split), high / len(split)))
        level = level * jnp.repeat(heights, dims[axis_at] // shards_of).reshape([-1 if axis == axis_at else 1 for axis in range(len(dims))])
    return level


def shared_out(key, own, number, rows, number_of, top, reach, lean):
    order = jax.random.permutation(key, number_of)
    packed, ordinary = portions_of(number_of, rows * top, reach, lean, True), portions_of(number_of, rows * top, reach, lean, False)
    places = jnp.arange(number_of)

    def named(lengths, rotation):
        used = int((lengths > 0).sum())
        fixed = max(1, used // 4)
        passed = fixed + (places - fixed + rotation * (used - fixed)) % max(1, number_of - fixed)
        return jnp.zeros((number_of,), jnp.int32).at[order[jnp.where(places < fixed, places, passed)]].set(jnp.asarray(lengths, jnp.int32))

    lengths = jnp.where(number % 4 == 0, named(packed, number // 4), named(ordinary, number - number // 4 - 1))
    mixed = jax.random.permutation(jax.random.fold_in(own, 3), number_of)
    giver, taker = mixed[0:number_of // 2 * 2:2], mixed[1:number_of // 2 * 2:2]
    margin = jnp.minimum(lengths[giver] - 1, reach - lengths[taker]) // 2
    margin = jnp.where((giver == order[0]) | (taker == order[0]) | (lengths[taker] == 0), 0, jnp.maximum(margin, 0))
    passed = jax.random.randint(jax.random.fold_in(own, 4), (number_of // 2,), 0, 1 << 20) % (margin + 1)
    lengths = lengths.at[giver].add(-passed).at[taker].add(passed)
    items = jnp.searchsorted(jnp.cumsum(lengths), jnp.arange(rows * top), side="right").astype(jnp.int32)
    grid = items.reshape(top, rows).T
    grid = grid[jax.random.permutation(jax.random.fold_in(own, 1), rows)]
    rotation = jax.random.randint(jax.random.fold_in(own, 2), (rows, 1), 0, top)
    return jnp.take_along_axis(grid, (jnp.arange(top)[None, :] + rotation) % top, axis=1)


def portions_of(number_of, total, most, slope, full):
    loads = [(1 << 20) // math.isqrt(rank ** slope) + 1 for rank in range(1, number_of + 1)]
    largest = most if full else min(most, max(-(-total // number_of), total * loads[0] // sum(loads)))
    least = 1 if total - largest >= number_of - 1 else 0
    holding, rest = [largest] + [least] * (number_of - 1), total - largest - least * (number_of - 1)
    while rest > 0:
        movable = [i for i in range(1, number_of) if holding[i] < largest] or [i for i in range(1, number_of) if holding[i] < most]
        pool, left = sum([loads[i] for i in movable]), rest
        for i in movable:
            extra = min(most - holding[i], max(1, left * loads[i] // pool), rest)
            holding[i] = holding[i] + extra
            rest = rest - extra
    return np.array(holding)


def bell_draw(own_key, extent, spread, most, shards=(), kind=jnp.bfloat16):
    drawn = jax.random.normal(own_key, extent, jnp.float32) * spread
    if len(shards) > 0:
        drawn = shard_levels(own_key, extent, shards, -0.22, 0.18) * drawn
    return jnp.clip(drawn, min=-most, max=most).astype(kind)


def setup_inputs(seed: int = 0) -> dict:
    keys = jax.random.split(jax.random.key(seed), 6)
    grad_out = bell_draw(keys[0], (TOKENS, D), 1.0, 6.0, ((0, 32),))
    saved_pre = bell_draw(keys[1], (TOKENS, TOP, 2 * HID), 1.5, 6.0, ((0, 32),))
    gate_weight = jnp.clip(0.049804688 + 0.54785156 * jax.random.uniform(keys[2], (TOKENS, TOP), jnp.float32) ** shard_levels(keys[2], (TOKENS, TOP), ((0, 32),), -0.2, 0.2), 0.049804688, 0.59765625).astype(jnp.bfloat16)
    routes_keys = jax.random.split(jax.random.fold_in(keys[3], 1), TOKENS // TOK_DEV)
    routes_turns = jax.random.permutation(jax.random.fold_in(keys[3], 3), TOKENS // TOK_DEV)
    routes = jax.vmap(lambda own, number: shared_out(jax.random.fold_in(keys[3], 2), own, number, TOK_DEV, EXPERTS, TOP, CAP, 2))(routes_keys, routes_turns).reshape((TOKENS, TOP))
    w_down = bell_draw(keys[4], (EXPERTS, HID, D), D ** -0.5, 0.09375, ((0, 16), (2, 2)))
    return {"grad_out": grad_out, "saved_pre": saved_pre, "gate_weight": gate_weight, "routes": routes, "w_down": w_down}


def slot_positions(routes_flat, experts, capacity):
    expert_ids = jnp.arange(experts, dtype=jnp.int32)
    onehot = (routes_flat[:, None] == expert_ids[None, :]).astype(jnp.int32)
    rank = jnp.sum((jnp.cumsum(onehot, axis=0) - 1) * onehot, axis=1)
    return (routes_flat * capacity + rank).astype(jnp.int32)


def swiglu_parts(saved, hidden):
    gate_pre = saved[..., :hidden].astype(jnp.float32)
    up_pre = saved[..., hidden:].astype(jnp.float32)
    return gate_pre, up_pre, jax.nn.silu(gate_pre)


def swiglu_grads(saved, weights, contraction, hidden):
    gate_pre, up_pre, active = swiglu_parts(saved, hidden)
    plain = lax.optimization_barrier((active * up_pre).astype(jnp.bfloat16))
    gate_grad = jnp.sum(plain.astype(jnp.float32) * contraction.astype(jnp.float32), axis=-1).astype(jnp.bfloat16)
    back = weights.astype(jnp.float32)[..., None] * contraction.astype(jnp.float32)
    sigma = jax.nn.sigmoid(gate_pre)
    grad_gate_pre = back * up_pre * sigma * (1.0 + gate_pre * (1.0 - sigma))
    grad_up_pre = back * active
    return jnp.concatenate([grad_gate_pre, grad_up_pre], axis=-1).astype(jnp.bfloat16), gate_grad


def scaled_hidden(saved, weights, hidden):
    gate_pre, up_pre, active = swiglu_parts(saved, hidden)
    return (weights.astype(jnp.float32)[..., None] * active * up_pre).astype(jnp.bfloat16)


def reference(grad_out, saved_pre, gate_weight, routes, w_down):
    devices = N_DP * N_EXPERT
    route_count = TOK_DEV * TOP
    per_device = routes.reshape(devices, route_count)
    positions = jax.vmap(lambda row: slot_positions(row, EXPERTS, CAP))(per_device)
    global_ids = jnp.arange(devices * route_count, dtype=jnp.int32).reshape(devices, route_count)
    owners = jnp.zeros((devices, EXPERTS * CAP), jnp.int32)
    owners = owners.at[jnp.arange(devices, dtype=jnp.int32)[:, None], positions].set(global_ids + 1)
    owners = owners.reshape(devices, EXPERTS, CAP).transpose(1, 0, 2).reshape(EXPERTS, devices * CAP)
    saved_flat = saved_pre.reshape(devices * route_count, 2 * HID)
    weight_flat = gate_weight.reshape(devices * route_count)

    def per_expert(item):
        owner_row, weights = item
        filled = owner_row > 0
        route_ids = jnp.maximum(owner_row - 1, 0)
        rows = jnp.where(filled[:, None], jnp.take(grad_out, route_ids // TOP, axis=0), 0)
        saved = jnp.where(filled[:, None], jnp.take(saved_flat, route_ids, axis=0), 0)
        route_weights = jnp.where(filled, jnp.take(weight_flat, route_ids), 0)
        contraction = jnp.dot(rows, weights.T, preferred_element_type=jnp.float32).astype(jnp.bfloat16)
        scaled = scaled_hidden(saved, route_weights, HID)
        gradient = jnp.dot(scaled.T, rows, preferred_element_type=jnp.float32).astype(jnp.bfloat16)
        return contraction, gradient

    contraction_all, grad_down = lax.map(per_expert, (owners, w_down))
    flat_routes = routes.reshape(devices * route_count)
    device_of = jnp.arange(devices * route_count, dtype=jnp.int32) // route_count
    slot_index = (device_of * CAP + (positions.reshape(devices * route_count) - flat_routes * CAP)).astype(jnp.int32)
    contraction = contraction_all[flat_routes, slot_index]
    grad_pre, grad_gate = swiglu_grads(saved_flat, weight_flat, contraction, HID)
    return grad_pre.reshape(TOKENS, TOP, 2 * HID), grad_gate.reshape(TOKENS, TOP), grad_down
```

```python
import jax
import jax.numpy as jnp
from jax import lax
from jax.sharding import PartitionSpec as P

BF16 = jnp.bfloat16
F32 = jnp.float32


def slot_positions(routes_flat, experts, capacity):
    expert_ids = jnp.arange(experts, dtype=jnp.int32)
    onehot = (routes_flat[:, None] == expert_ids[None, :]).astype(jnp.int32)
    rank = jnp.sum((jnp.cumsum(onehot, axis=0) - 1) * onehot, axis=1)
    return routes_flat * capacity + rank


def swiglu_parts(saved, hidden):
    gate_pre = saved[..., :hidden].astype(F32)
    up_pre = saved[..., hidden:].astype(F32)
    return (gate_pre, up_pre, jax.nn.silu(gate_pre))


def swiglu_grads(saved, weights, contraction, hidden):
    gate_pre, up_pre, active = swiglu_parts(saved, hidden)
    plain = (active * up_pre).astype(BF16)
    gate_grad = jnp.sum(plain.astype(F32) * contraction.astype(F32), axis=-1).astype(BF16)
    back = weights.astype(F32)[..., None] * contraction.astype(F32)
    sigma = jax.nn.sigmoid(gate_pre)
    grad_gate_pre = back * up_pre * sigma * (1.0 + gate_pre * (1.0 - sigma))
    grad_up_pre = back * active
    return (jnp.concatenate([grad_gate_pre, grad_up_pre], axis=-1).astype(BF16), gate_grad)


def scaled_hidden(saved, weights, hidden):
    gate_pre, up_pre, active = swiglu_parts(saved, hidden)
    return (weights.astype(F32)[..., None] * active * up_pre).astype(BF16)


def dot(a, b, dims):
    return lax.dot_general(a, b, (dims, ((), ())), preferred_element_type=F32)


def on_device(grad_out, saved_pre, gate_weight, routes, w_down):
    tokens_dev, top_count = routes.shape
    hidden = w_down.shape[1]
    half = w_down.shape[2]
    experts = lax.axis_size("expert")
    replicas = lax.axis_size("dp")
    capacity = 5 * tokens_dev * top_count // (4 * experts)
    slots = experts * capacity
    positions = slot_positions(routes.reshape(-1), experts, capacity).reshape(tokens_dev, top_count)
    slot_ids = jnp.arange(slots, dtype=jnp.int32)
    picks = [
        (positions[:, k][None, :] == slot_ids[:, None]).astype(BF16) for k in range(top_count)
    ]
    pick = sum(picks[1:], picks[0])
    devices = replicas * experts
    send_rows = jnp.stack(
        [
            dot(pick, grad_out[:, d * half : (d + 1) * half], ((1,), (0,))).astype(BF16)
            for d in range(replicas)
        ]
    ).reshape(devices, capacity, half)
    scaled = scaled_hidden(saved_pre, gate_weight, hidden)
    send_scaled = sum(dot(picks[k], scaled[:, k], ((1,), (0,))) for k in range(top_count))
    send_scaled = send_scaled.astype(BF16).reshape(experts, capacity, hidden)
    rows = lax.all_to_all(send_rows, ("dp", "expert"), split_axis=0, concat_axis=0, tiled=True)
    scaled_in = lax.all_to_all(send_scaled, "expert", split_axis=0, concat_axis=0, tiled=True)
    scaled_in = lax.all_gather(scaled_in.reshape(slots, hidden), "dp", axis=0, tiled=True)
    rows = rows.reshape(devices * capacity, half)
    partial = dot(rows, w_down[0], ((1,), (1,))).astype(BF16).reshape(devices, capacity, hidden)
    parts = lax.all_to_all(partial, ("dp", "expert"), split_axis=0, concat_axis=0, tiled=True)
    parts = parts.reshape(replicas, slots, hidden)
    contraction = jnp.stack(
        [
            sum(dot(picks[k], parts[d], ((0,), (0,))) for d in range(replicas))
            for k in range(top_count)
        ],
        axis=1,
    ).astype(BF16)
    grads, gate_grad = swiglu_grads(saved_pre, gate_weight, contraction, hidden)
    grad_down = dot(scaled_in, rows, ((0,), (0,))).astype(BF16)
    return grads, gate_grad, grad_down[None]


def solution(mesh):
    return jax.shard_map(
        on_device,
        mesh=mesh,
        in_specs=(
            P(("dp", "expert"), None),
            P(("dp", "expert"), None, None),
            P(("dp", "expert"), None),
            P(("dp", "expert"), None),
            P("expert", None, "dp"),
        ),
        out_specs=(
            P(("dp", "expert"), None, None),
            P(("dp", "expert"), None),
            P("expert", None, "dp"),
        ),
        check_vma=False,
    )
```

```python
import functools

import jax
import jax.numpy as jnp
from jax import lax
from jax.experimental import pallas as pl
from jax.experimental.pallas import tpu as pltpu
from jax.sharding import PartitionSpec as P

BF16 = jnp.bfloat16
F32 = jnp.float32


def slot_positions(routes_flat, experts, capacity):
    expert_ids = jnp.arange(experts, dtype=jnp.int32)
    onehot = (routes_flat[:, None] == expert_ids[None, :]).astype(jnp.int32)
    rank = jnp.sum((jnp.cumsum(onehot, axis=0) - 1) * onehot, axis=1)
    return routes_flat * capacity + rank


def swiglu_parts(saved, hidden):
    gate_pre = saved[..., :hidden].astype(F32)
    up_pre = saved[..., hidden:].astype(F32)
    return (gate_pre, up_pre, jax.nn.silu(gate_pre))


def swiglu_grads(saved, weights, contraction, hidden):
    gate_pre, up_pre, active = swiglu_parts(saved, hidden)
    plain = (active * up_pre).astype(BF16)
    gate_grad = jnp.sum(plain.astype(F32) * contraction.astype(F32), axis=-1).astype(BF16)
    back = weights.astype(F32)[..., None] * contraction.astype(F32)
    sigma = jax.nn.sigmoid(gate_pre)
    grad_gate_pre = back * up_pre * sigma * (1.0 + gate_pre * (1.0 - sigma))
    grad_up_pre = back * active
    return (jnp.concatenate([grad_gate_pre, grad_up_pre], axis=-1).astype(BF16), gate_grad)


def scaled_hidden(saved, weights, hidden):
    gate_pre, up_pre, active = swiglu_parts(saved, hidden)
    return (weights.astype(F32)[..., None] * active * up_pre).astype(BF16)


def dot(a, b, dims):
    return lax.dot_general(a, b, (dims, ((), ())), preferred_element_type=F32)


def on_device_general(grad_out, saved_pre, gate_weight, routes, w_down):
    tokens_dev, top_count = routes.shape
    hidden = w_down.shape[1]
    half = w_down.shape[2]
    experts = lax.axis_size("expert")
    replicas = lax.axis_size("dp")
    capacity = 5 * tokens_dev * top_count // (4 * experts)
    slots = experts * capacity
    positions = slot_positions(routes.reshape(-1), experts, capacity).reshape(tokens_dev, top_count)
    slot_ids = jnp.arange(slots, dtype=jnp.int32)
    picks = [
        (positions[:, k][None, :] == slot_ids[:, None]).astype(BF16) for k in range(top_count)
    ]
    pick = sum(picks[1:], picks[0])
    devices = replicas * experts
    send_rows = jnp.stack(
        [
            dot(pick, grad_out[:, d * half : (d + 1) * half], ((1,), (0,))).astype(BF16)
            for d in range(replicas)
        ]
    ).reshape(devices, capacity, half)
    scaled = scaled_hidden(saved_pre, gate_weight, hidden)
    send_scaled = sum(dot(picks[k], scaled[:, k], ((1,), (0,))) for k in range(top_count))
    send_scaled = send_scaled.astype(BF16).reshape(experts, capacity, hidden)
    rows = lax.all_to_all(send_rows, ("dp", "expert"), split_axis=0, concat_axis=0, tiled=True)
    scaled_in = lax.all_to_all(send_scaled, "expert", split_axis=0, concat_axis=0, tiled=True)
    scaled_in = lax.all_gather(scaled_in.reshape(slots, hidden), "dp", axis=0, tiled=True)
    rows = rows.reshape(devices * capacity, half)
    partial = dot(rows, w_down[0], ((1,), (1,))).astype(BF16).reshape(devices, capacity, hidden)
    parts = lax.all_to_all(partial, ("dp", "expert"), split_axis=0, concat_axis=0, tiled=True)
    parts = parts.reshape(replicas, slots, hidden)
    contraction = jnp.stack(
        [
            sum(dot(picks[k], parts[d], ((0,), (0,))) for d in range(replicas))
            for k in range(top_count)
        ],
        axis=1,
    ).astype(BF16)
    grads, gate_grad = swiglu_grads(saved_pre, gate_weight, contraction, hidden)
    grad_down = dot(scaled_in, rows, ((0,), (0,))).astype(BF16)
    return grads, gate_grad, grad_down[None]


BASE = 16
MESH = pl.DeviceIdType.MESH


def iota(shape, axis):
    return lax.broadcasted_iota(jnp.int32, shape, axis)


def unfold_pick(groups, rest, fold, q):
    shape = (groups * rest, groups * BASE)
    row, col = iota(shape, 0), iota(shape, 1)
    return (col == (row // rest) * BASE + q * rest + row % rest).astype(BF16)


def fold_pick(groups, rest, fold, q):
    shape = (groups * BASE, groups * rest)
    row, col = iota(shape, 0), iota(shape, 1)
    mine = (row // rest) % fold == q
    return (mine & (col == (row // BASE) * rest + row % rest)).astype(BF16)


def pack_kernel(experts, rest, fold, replicas, s_fold, pos, rows, scaled0, scaled1, main, left, smain, sleft):
    tokens, width = rows.shape
    half = width // replicas
    part = half // fold
    count = experts * BASE
    pos0, pos1 = pos[0:1, :], pos[1:2, :]
    row = iota((count, tokens), 0)
    pick0, pick1 = (pos0 == row).astype(BF16), (pos1 == row).astype(BF16)
    both = pick0 + pick1
    step = 1024
    for c in range(0, width, step):
        main[:, c : c + step] = dot(both, rows[:, c : c + step], ((1,), (0,))).astype(BF16)
    smain[...] = (
        dot(pick0, scaled0[...], ((1,), (0,))) + dot(pick1, scaled1[...], ((1,), (0,)))
    ).astype(BF16)
    slot = count + (row // BASE) * rest + row % rest
    total = [jnp.zeros((count, part), F32) for _ in range(replicas)]
    part_s = sleft.shape[1]
    total_s = jnp.zeros((count, part_s), F32)
    for q in range(fold):
        mine = (row // rest) % fold == q
        q0, q1 = ((pos0 == slot) & mine).astype(BF16), ((pos1 == slot) & mine).astype(BF16)
        for d in range(replicas):
            at = d * half + q * part
            total[d] = total[d] + dot(q0 + q1, rows[:, at : at + part], ((1,), (0,)))
        if q < s_fold:
            at = q * part_s
            total_s = total_s + dot(q0, scaled0[:, at : at + part_s], ((1,), (0,)))
            total_s = total_s + dot(q1, scaled1[:, at : at + part_s], ((1,), (0,)))
    for d in range(replicas):
        left[:, d * part : (d + 1) * part] = total[d].astype(BF16)
    sleft[...] = total_s.astype(BF16)


def exchange_kernel(
    experts, rest, fold, s_fold,
    main, left, smain, sleft, w_hbm,
    ret_out, grad_out,
    w, x_main, x_left, z, s_main, s_left, s_rest, s_turn, s_turn_rest,
    mine_f32, out_px, in_px, out_pl, in_pl, c_main, c_left, r_main, r_left,
    w_sem, tx, rx, txl, rxl, ts, rs, tsl, rsl, tp, rp, tc, rc, tcl, rcl,
):
    d = lax.axis_index("dp")
    e = lax.axis_index("expert")
    other = 1 - d
    devices = 2 * experts
    me = d * experts + e
    half = w.shape[1]
    part = half // fold
    hidden = w.shape[0]
    part_s = sleft.shape[1]
    own, rest_own = experts * BASE, experts * rest

    def block(i):
        return pl.ds(pl.multiple_of(i * BASE, BASE), BASE)

    def remote(src, dst, send, recv, to):
        return pltpu.make_async_remote_copy(
            src_ref=src, dst_ref=dst, send_sem=send, recv_sem=recv, device_id=to, device_id_type=MESH
        )

    def row_copies(p, s):
        pd, pe = p // experts, p % experts
        wide = pl.ds(pl.multiple_of(pd * half, 128), half)
        narrow = pl.ds(pl.multiple_of(pd * part, 128), part)
        return (
            remote(main.at[block(pe), wide], x_main.at[block(s)], tx.at[p], rx.at[s], (pd, pe)),
            remote(left.at[block(pe), narrow], x_left.at[block(s)], txl.at[p], rxl.at[s], (pd, pe)),
        )

    def scaled_copies(pe, se):
        s = d * experts + se
        return (
            remote(smain.at[block(pe)], s_main.at[block(s)], ts.at[pe], rs.at[se], (d, pe)),
            remote(sleft.at[block(pe)], s_left.at[block(s)], tsl.at[pe], rsl.at[se], (d, pe)),
        )

    def back_copies(pe, se):
        return (
            remote(c_main.at[block(pe)], r_main.at[block(se)], tc.at[pe], rc.at[se], (d, pe)),
            remote(c_left.at[block(pe)], r_left.at[block(se)], tcl.at[pe], rcl.at[se], (d, pe)),
        )

    def each(count, position, body):
        def step(k, carry):
            body((position + k) % count)
            return carry

        lax.fori_loop(1, count, step, 0)

    fetch_w = pltpu.make_async_copy(w_hbm, w, w_sem)
    fetch_w.start()
    barrier = pltpu.get_barrier_semaphore()

    def greet(p):
        pl.semaphore_signal(
            barrier, inc=1, device_id=(p // experts, p % experts), device_id_type=MESH
        )

    each(devices, me, greet)
    pl.semaphore_wait(barrier, devices - 1)

    def start_rows(p):
        for copy in row_copies(p, me):
            copy.start()

    each(devices, me, start_rows)

    def start_scaled(p):
        for copy in scaled_copies(p, e):
            copy.start()

    each(experts, e, start_scaled)
    kept = [
        pltpu.make_async_copy(
            main.at[block(e), pl.ds(pl.multiple_of(d * half, 128), half)], x_main.at[block(me)], rx.at[me]
        ),
        pltpu.make_async_copy(
            left.at[block(e), pl.ds(pl.multiple_of(d * part, 128), part)], x_left.at[block(me)], rxl.at[me]
        ),
        pltpu.make_async_copy(smain.at[block(e)], s_main.at[block(me)], rs.at[e]),
        pltpu.make_async_copy(sleft.at[block(e)], s_left.at[block(me)], rsl.at[e]),
    ]
    for copy in kept:
        copy.start()
    for copy in kept:
        copy.wait()
    fetch_w.wait()

    def wait_rows(s):
        for copy in row_copies(s, s):
            copy.wait_recv()

    each(devices, me, wait_rows)

    for q in range(fold):
        z[:, q * part : (q + 1) * part] = dot(
            unfold_pick(devices, rest, fold, q), x_left[...], ((1,), (0,))
        ).astype(BF16)

    def contract(lo, ref, rows, start):
        return dot(ref[pl.ds(start, rows), :], w[lo : lo + 256, :], ((1,), (1,)))

    other_at, own_at = pl.multiple_of(other * own, own), pl.multiple_of(d * own, own)
    other_rest, own_rest = pl.multiple_of(other * rest_own, rest_own), pl.multiple_of(d * rest_own, rest_own)
    for lo in range(0, hidden, 256):
        out_px[:, lo : lo + 256] = contract(lo, x_main, own, other_at).astype(BF16)
        out_pl[:, lo : lo + 256] = contract(lo, z, rest_own, other_rest).astype(BF16)
    across = (other, e)
    px = remote(out_px, in_px, tp.at[0], rp.at[0], across)
    plx = remote(out_pl, in_pl, tp.at[1], rp.at[1], across)
    px.start()
    plx.start()
    for lo in range(0, hidden, 256):
        mine_f32[0:own, lo : lo + 256] = contract(lo, x_main, own, own_at)
        mine_f32[own : own + rest_own, lo : lo + 256] = contract(lo, z, rest_own, own_rest)
    px.wait()
    plx.wait()
    c_main[...] = (mine_f32[0:own, :] + in_px[...].astype(F32)).astype(BF16)
    c_rest = (mine_f32[own : own + rest_own, :] + in_pl[...].astype(F32)).astype(BF16)
    folded = jnp.zeros((own, part_s), F32)
    for q in range(s_fold):
        folded = folded + dot(
            fold_pick(experts, rest, fold, q), c_rest[:, q * part_s : (q + 1) * part_s], ((1,), (0,))
        )
    c_left[...] = folded.astype(BF16)

    def start_back(p):
        for copy in back_copies(p, e):
            copy.start()

    each(experts, e, start_back)
    kept_back = [
        pltpu.make_async_copy(c_main.at[block(e)], r_main.at[block(e)], rc.at[e]),
        pltpu.make_async_copy(c_left.at[block(e)], r_left.at[block(e)], rcl.at[e]),
    ]
    for copy in kept_back:
        copy.start()

    def wait_scaled(s):
        for copy in scaled_copies(s, s):
            copy.wait_recv()

    each(experts, e, wait_scaled)
    region = pl.ds(own_at, own)
    forward = [
        remote(s_main.at[region], s_main.at[region], tp.at[2], rp.at[2], across),
        remote(s_left.at[region], s_left.at[region], tp.at[3], rp.at[3], across),
    ]
    for copy in forward:
        copy.start()
    for copy in forward:
        copy.wait()
    for q in range(s_fold):
        s_rest[:, q * part_s : (q + 1) * part_s] = dot(
            unfold_pick(devices, rest, fold, q), s_left[...], ((1,), (0,))
        ).astype(BF16)
    s_turn[...] = s_main[...].T
    s_turn_rest[...] = s_rest[...].T

    @pl.loop(0, half // 512)
    def _(j):
        columns = pl.ds(pl.multiple_of(j * 512, 512), 512)
        grad_out[:, columns] = (
            dot(s_turn[...], x_main[:, columns], ((1,), (0,)))
            + dot(s_turn_rest[...], z[:, columns], ((1,), (0,)))
        ).astype(BF16)

    for copy in kept_back:
        copy.wait()

    def wait_back(s):
        for copy in back_copies(s, s):
            copy.wait_recv()

    each(experts, e, wait_back)
    ret_out[0:own, :] = r_main[...]
    for q in range(s_fold):
        ret_out[own : own + rest_own, q * part_s : (q + 1) * part_s] = dot(
            unfold_pick(experts, rest, fold, q), r_left[...], ((1,), (0,))
        ).astype(BF16)

    def drain_rows(p):
        for copy in row_copies(p, me):
            copy.wait_send()

    each(devices, me, drain_rows)

    def drain(p):
        for copy in scaled_copies(p, e) + back_copies(p, e):
            copy.wait_send()

    each(experts, e, drain)


def on_device(grad_out, saved_pre, gate_weight, routes, w_down):
    tokens, top_count = routes.shape
    hidden, half = w_down.shape[1:]
    width = grad_out.shape[1]
    experts = lax.axis_size("expert")
    replicas = lax.axis_size("dp")
    capacity = 5 * tokens * top_count // (4 * experts)
    if (replicas, top_count, capacity, hidden % 256, half % 512) != (2, 2, 20, 0, 0):
        return on_device_general(grad_out, saved_pre, gate_weight, routes, w_down)
    rest = capacity - BASE
    fold = BASE // rest
    s_fold = hidden // 256
    own, rest_own = experts * BASE, experts * rest
    devices = replicas * experts
    expert_ids = jnp.arange(experts, dtype=jnp.int32)
    named = [(routes[:, k][:, None] == expert_ids[None, :]).astype(F32) for k in range(2)]
    before = (jnp.arange(tokens)[:, None] > jnp.arange(tokens)[None, :]).astype(BF16)
    counts = dot(before, (named[0] + named[1]).astype(BF16), ((1,), (0,)))
    positions = []
    for k in range(2):
        rank = jnp.sum(counts * named[k], axis=1).astype(jnp.int32)
        expert = routes[:, k]
        positions.append(
            jnp.where(rank < BASE, expert * BASE + rank, own + expert * rest + rank - BASE)
        )
    scaled = [
        scaled_hidden(saved_pre[:, k], gate_weight[:, k], hidden) for k in range(2)
    ]
    vmem = pl.BlockSpec(memory_space=pltpu.VMEM)
    packed = pl.pallas_call(
        functools.partial(pack_kernel, experts, rest, fold, replicas, s_fold),
        out_shape=(
            jax.ShapeDtypeStruct((own, width), BF16),
            jax.ShapeDtypeStruct((own, width // fold), BF16),
            jax.ShapeDtypeStruct((own, hidden), BF16),
            jax.ShapeDtypeStruct((own, 256), BF16),
        ),
        in_specs=[vmem] * 4,
        out_specs=[vmem] * 4,
    )(jnp.stack(positions), grad_out, scaled[0], scaled[1])
    dma = pltpu.SemaphoreType.DMA
    total = devices * BASE
    back, grad_down = pl.pallas_call(
        functools.partial(exchange_kernel, experts, rest, fold, s_fold),
        out_shape=(
            jax.ShapeDtypeStruct((own + rest_own, hidden), BF16),
            jax.ShapeDtypeStruct((hidden, half), BF16),
        ),
        in_specs=[vmem] * 4 + [pl.BlockSpec(memory_space=pl.ANY)],
        out_specs=[vmem] * 2,
        scratch_shapes=[
            pltpu.VMEM((hidden, half), BF16),
            pltpu.VMEM((total, half), BF16),
            pltpu.VMEM((total, half // fold), BF16),
            pltpu.VMEM((devices * rest, half), BF16),
            pltpu.VMEM((total, hidden), BF16),
            pltpu.VMEM((total, 256), BF16),
            pltpu.VMEM((devices * rest, hidden), BF16),
            pltpu.VMEM((hidden, total), BF16),
            pltpu.VMEM((hidden, devices * rest), BF16),
            pltpu.VMEM((own + rest_own, hidden), F32),
            pltpu.VMEM((own, hidden), BF16),
            pltpu.VMEM((own, hidden), BF16),
            pltpu.VMEM((rest_own, hidden), BF16),
            pltpu.VMEM((rest_own, hidden), BF16),
            pltpu.VMEM((own, hidden), BF16),
            pltpu.VMEM((own, 256), BF16),
            pltpu.VMEM((own, hidden), BF16),
            pltpu.VMEM((own, 256), BF16),
            dma,
            dma((devices,)), dma((devices,)), dma((devices,)), dma((devices,)),
            dma((experts,)), dma((experts,)), dma((experts,)), dma((experts,)),
            dma((4,)), dma((4,)),
            dma((experts,)), dma((experts,)), dma((experts,)), dma((experts,)),
        ],
        compiler_params=pltpu.CompilerParams(collective_id=0, has_side_effects=True),
    )(*packed, w_down[0])
    slot_ids = jnp.arange(own + rest_own, dtype=jnp.int32)
    contraction = jnp.stack(
        [
            dot((positions[k][:, None] == slot_ids[None, :]).astype(BF16), back, ((1,), (0,))).astype(BF16)
            for k in range(2)
        ],
        axis=1,
    )
    grads, gate_grad = swiglu_grads(saved_pre, gate_weight, contraction, hidden)
    return grads, gate_grad, grad_down[None]


def solution(mesh):
    return jax.shard_map(
        on_device,
        mesh=mesh,
        in_specs=(
            P(("dp", "expert"), None),
            P(("dp", "expert"), None, None),
            P(("dp", "expert"), None),
            P(("dp", "expert"), None),
            P("expert", None, "dp"),
        ),
        out_specs=(
            P(("dp", "expert"), None, None),
            P(("dp", "expert"), None),
            P("expert", None, "dp"),
        ),
        check_vma=False,
    )
```

```python
import functools

import jax
import jax.numpy as jnp
from jax import lax
from jax.experimental import pallas as pl
from jax.experimental.pallas import tpu as pltpu
from jax.sharding import PartitionSpec as P

BF16 = jnp.bfloat16
F32 = jnp.float32


def slot_positions(routes_flat, experts, capacity):
    expert_ids = jnp.arange(experts, dtype=jnp.int32)
    onehot = (routes_flat[:, None] == expert_ids[None, :]).astype(jnp.int32)
    rank = jnp.sum((jnp.cumsum(onehot, axis=0) - 1) * onehot, axis=1)
    return routes_flat * capacity + rank


def swiglu_parts(saved, hidden):
    gate_pre = saved[..., :hidden].astype(F32)
    up_pre = saved[..., hidden:].astype(F32)
    return (gate_pre, up_pre, jax.nn.silu(gate_pre))


def swiglu_grads(saved, weights, contraction, hidden):
    gate_pre, up_pre, active = swiglu_parts(saved, hidden)
    plain = (active * up_pre).astype(BF16)
    gate_grad = jnp.sum(plain.astype(F32) * contraction.astype(F32), axis=-1).astype(BF16)
    back = weights.astype(F32)[..., None] * contraction.astype(F32)
    sigma = jax.nn.sigmoid(gate_pre)
    grad_gate_pre = back * up_pre * sigma * (1.0 + gate_pre * (1.0 - sigma))
    grad_up_pre = back * active
    return (jnp.concatenate([grad_gate_pre, grad_up_pre], axis=-1).astype(BF16), gate_grad)


def scaled_hidden(saved, weights, hidden):
    gate_pre, up_pre, active = swiglu_parts(saved, hidden)
    return (weights.astype(F32)[..., None] * active * up_pre).astype(BF16)


def dot(a, b, dims):
    return lax.dot_general(a, b, (dims, ((), ())), preferred_element_type=F32)


def on_device_general(grad_out, saved_pre, gate_weight, routes, w_down):
    tokens_dev, top_count = routes.shape
    hidden = w_down.shape[1]
    half = w_down.shape[2]
    experts = lax.axis_size("expert")
    replicas = lax.axis_size("dp")
    capacity = 5 * tokens_dev * top_count // (4 * experts)
    slots = experts * capacity
    positions = slot_positions(routes.reshape(-1), experts, capacity).reshape(tokens_dev, top_count)
    slot_ids = jnp.arange(slots, dtype=jnp.int32)
    picks = [
        (positions[:, k][None, :] == slot_ids[:, None]).astype(BF16) for k in range(top_count)
    ]
    pick = sum(picks[1:], picks[0])
    devices = replicas * experts
    send_rows = jnp.stack(
        [
            dot(pick, grad_out[:, d * half : (d + 1) * half], ((1,), (0,))).astype(BF16)
            for d in range(replicas)
        ]
    ).reshape(devices, capacity, half)
    scaled = scaled_hidden(saved_pre, gate_weight, hidden)
    send_scaled = sum(dot(picks[k], scaled[:, k], ((1,), (0,))) for k in range(top_count))
    send_scaled = send_scaled.astype(BF16).reshape(experts, capacity, hidden)
    rows = lax.all_to_all(send_rows, ("dp", "expert"), split_axis=0, concat_axis=0, tiled=True)
    scaled_in = lax.all_to_all(send_scaled, "expert", split_axis=0, concat_axis=0, tiled=True)
    scaled_in = lax.all_gather(scaled_in.reshape(slots, hidden), "dp", axis=0, tiled=True)
    rows = rows.reshape(devices * capacity, half)
    partial = dot(rows, w_down[0], ((1,), (1,))).astype(BF16).reshape(devices, capacity, hidden)
    parts = lax.all_to_all(partial, ("dp", "expert"), split_axis=0, concat_axis=0, tiled=True)
    parts = parts.reshape(replicas, slots, hidden)
    contraction = jnp.stack(
        [
            sum(dot(picks[k], parts[d], ((0,), (0,))) for d in range(replicas))
            for k in range(top_count)
        ],
        axis=1,
    ).astype(BF16)
    grads, gate_grad = swiglu_grads(saved_pre, gate_weight, contraction, hidden)
    grad_down = dot(scaled_in, rows, ((0,), (0,))).astype(BF16)
    return grads, gate_grad, grad_down[None]


BASE = 16
MESH = pl.DeviceIdType.MESH


def iota(shape, axis):
    return lax.broadcasted_iota(jnp.int32, shape, axis)


def unfold_pick(groups, rest, fold, q):
    shape = (groups * rest, groups * BASE)
    row, col = iota(shape, 0), iota(shape, 1)
    return (col == (row // rest) * BASE + q * rest + row % rest).astype(BF16)


def fold_pick(groups, rest, fold, q):
    shape = (groups * BASE, groups * rest)
    row, col = iota(shape, 0), iota(shape, 1)
    mine = (row // rest) % fold == q
    return (mine & (col == (row // BASE) * rest + row % rest)).astype(BF16)


def pack_kernel(
    experts, rest, fold, replicas, s_fold,
    routes, rows, scaled0, scaled1,
    main, left, smain, sleft, pos,
):
    tokens, width = rows.shape
    half = width // replicas
    part = half // fold
    count = experts * BASE
    names = iota((experts, tokens), 0)
    named = [(routes[k : k + 1, :] == names).astype(F32) for k in range(2)]
    before = (iota((tokens, tokens), 0) < iota((tokens, tokens), 1)).astype(BF16)
    counts = dot((named[0] + named[1]).astype(BF16), before, ((1,), (0,)))
    for k in range(2):
        rank = jnp.sum(counts * named[k], axis=0, keepdims=True).astype(jnp.int32)
        expert = routes[k : k + 1, :]
        pos[k : k + 1, :] = jnp.where(
            rank < BASE, expert * BASE + rank, count + expert * rest + rank - BASE
        )
    pos0, pos1 = pos[0:1, :], pos[1:2, :]
    row = iota((count, tokens), 0)
    pick0, pick1 = (pos0 == row).astype(BF16), (pos1 == row).astype(BF16)
    both = pick0 + pick1
    step = 1024
    for c in range(0, width, step):
        main[:, c : c + step] = dot(both, rows[:, c : c + step], ((1,), (0,))).astype(BF16)
    smain[...] = (
        dot(pick0, scaled0[...], ((1,), (0,))) + dot(pick1, scaled1[...], ((1,), (0,)))
    ).astype(BF16)
    slot = count + (row // BASE) * rest + row % rest
    total = [jnp.zeros((count, part), F32) for _ in range(replicas)]
    part_s = sleft.shape[1]
    total_s = jnp.zeros((count, part_s), F32)
    for q in range(fold):
        mine = (row // rest) % fold == q
        q0, q1 = ((pos0 == slot) & mine).astype(BF16), ((pos1 == slot) & mine).astype(BF16)
        for d in range(replicas):
            at = d * half + q * part
            total[d] = total[d] + dot(q0 + q1, rows[:, at : at + part], ((1,), (0,)))
        if q < s_fold:
            at = q * part_s
            total_s = total_s + dot(q0, scaled0[:, at : at + part_s], ((1,), (0,)))
            total_s = total_s + dot(q1, scaled1[:, at : at + part_s], ((1,), (0,)))
    for d in range(replicas):
        left[:, d * part : (d + 1) * part] = total[d].astype(BF16)
    sleft[...] = total_s.astype(BF16)


def exchange_kernel(
    experts, rest, fold, s_fold,
    main, left, smain, sleft, w_hbm,
    ret_out, grad_out,
    w, x_main, x_left, z, s_main, s_left, s_rest, s_turn, s_turn_rest,
    mine_f32, out_px, in_px, out_pl, in_pl, c_main, c_left, r_main, r_left,
    w_sem, tx, rx, txl, rxl, ts, rs, tsl, rsl, tp, rp, tc, rc, tcl, rcl,
):
    d = lax.axis_index("dp")
    e = lax.axis_index("expert")
    other = 1 - d
    devices = 2 * experts
    me = d * experts + e
    half = w.shape[1]
    part = half // fold
    hidden = w.shape[0]
    part_s = sleft.shape[1]
    own, rest_own = experts * BASE, experts * rest

    def block(i):
        return pl.ds(pl.multiple_of(i * BASE, BASE), BASE)

    def remote(src, dst, send, recv, to):
        return pltpu.make_async_remote_copy(
            src_ref=src, dst_ref=dst, send_sem=send, recv_sem=recv, device_id=to, device_id_type=MESH
        )

    def row_copies(p, s):
        pd, pe = p // experts, p % experts
        wide = pl.ds(pl.multiple_of(pd * half, 128), half)
        narrow = pl.ds(pl.multiple_of(pd * part, 128), part)
        return (
            remote(main.at[block(pe), wide], x_main.at[block(s)], tx.at[p], rx.at[s], (pd, pe)),
            remote(left.at[block(pe), narrow], x_left.at[block(s)], txl.at[p], rxl.at[s], (pd, pe)),
        )

    def scaled_copies(pe, se):
        s = d * experts + se
        return (
            remote(smain.at[block(pe)], s_main.at[block(s)], ts.at[pe], rs.at[se], (d, pe)),
            remote(sleft.at[block(pe)], s_left.at[block(s)], tsl.at[pe], rsl.at[se], (d, pe)),
        )

    def back_copies(pe, se):
        return (
            remote(c_main.at[block(pe)], r_main.at[block(se)], tc.at[pe], rc.at[se], (d, pe)),
            remote(c_left.at[block(pe)], r_left.at[block(se)], tcl.at[pe], rcl.at[se], (d, pe)),
        )

    def each(count, position, body):
        def step(k, carry):
            body((position + 1 + (k + count // 2 - 1) % (count - 1)) % count)
            return carry

        lax.fori_loop(1, count, step, 0)

    fetch_w = pltpu.make_async_copy(w_hbm, w, w_sem)
    fetch_w.start()
    barrier = pltpu.get_barrier_semaphore()

    def greet(p):
        pl.semaphore_signal(
            barrier, inc=1, device_id=(p // experts, p % experts), device_id_type=MESH
        )

    each(devices, me, greet)
    pl.semaphore_wait(barrier, devices - 1)

    def start_across(k, carry):
        for copy in row_copies(other * experts + (e + experts // 2 + k) % experts, me):
            copy.start()
        return carry

    lax.fori_loop(0, experts, start_across, 0)

    def start_scaled(p):
        for copy in scaled_copies(p, e):
            copy.start()

    each(experts, e, start_scaled)

    def start_rows(p):
        for copy in row_copies(d * experts + p, me):
            copy.start()

    each(experts, e, start_rows)
    kept = [
        pltpu.make_async_copy(
            main.at[block(e), pl.ds(pl.multiple_of(d * half, 128), half)], x_main.at[block(me)], rx.at[me]
        ),
        pltpu.make_async_copy(
            left.at[block(e), pl.ds(pl.multiple_of(d * part, 128), part)], x_left.at[block(me)], rxl.at[me]
        ),
        pltpu.make_async_copy(smain.at[block(e)], s_main.at[block(me)], rs.at[e]),
        pltpu.make_async_copy(sleft.at[block(e)], s_left.at[block(me)], rsl.at[e]),
    ]
    for copy in kept:
        copy.start()
    for copy in kept:
        copy.wait()
    fetch_w.wait()

    other_at, own_at = pl.multiple_of(other * own, own), pl.multiple_of(d * own, own)
    other_rest, own_rest = pl.multiple_of(other * rest_own, rest_own), pl.multiple_of(d * rest_own, rest_own)

    def unfold_rows(at, rest_at):
        for q in range(fold):
            z[pl.ds(rest_at, rest_own), q * part : (q + 1) * part] = dot(
                unfold_pick(experts, rest, fold, q), x_left[pl.ds(at, own), :], ((1,), (0,))
            ).astype(BF16)

    def contract(lo, ref, rows, start):
        return dot(ref[pl.ds(start, rows), :], w[lo : lo + 256, :], ((1,), (1,)))

    def wait_across(k, carry):
        s = other * experts + k
        for copy in row_copies(s, s):
            copy.wait_recv()
        return carry

    lax.fori_loop(0, experts, wait_across, 0)
    unfold_rows(other_at, other_rest)
    for lo in range(0, hidden, 256):
        out_px[:, lo : lo + 256] = contract(lo, x_main, own, other_at).astype(BF16)
        out_pl[:, lo : lo + 256] = contract(lo, z, rest_own, other_rest).astype(BF16)
    across = (other, e)
    px = remote(out_px, in_px, tp.at[0], rp.at[0], across)
    plx = remote(out_pl, in_pl, tp.at[1], rp.at[1], across)
    px.start()
    plx.start()

    def wait_scaled(s):
        for copy in scaled_copies(s, s):
            copy.wait_recv()

    each(experts, e, wait_scaled)
    region = pl.ds(own_at, own)
    forward = [
        remote(s_main.at[region], s_main.at[region], tp.at[2], rp.at[2], across),
        remote(s_left.at[region], s_left.at[region], tp.at[3], rp.at[3], across),
    ]
    for copy in forward:
        copy.start()
    px.wait()
    plx.wait()
    for copy in forward:
        copy.wait()
    for q in range(s_fold):
        s_rest[:, q * part_s : (q + 1) * part_s] = dot(
            unfold_pick(devices, rest, fold, q), s_left[...], ((1,), (0,))
        ).astype(BF16)
    s_turn[...] = s_main[...].T
    s_turn_rest[...] = s_rest[...].T

    def wait_rows(p):
        s = d * experts + p
        for copy in row_copies(s, s):
            copy.wait_recv()

    each(experts, e, wait_rows)
    unfold_rows(own_at, own_rest)
    for lo in range(0, hidden, 256):
        cut = slice(lo, lo + 256)
        c_main[:, cut] = (contract(lo, x_main, own, own_at) + in_px[:, cut].astype(F32)).astype(BF16)
        mine_f32[:, cut] = contract(lo, z, rest_own, own_rest)
    c_rest = (mine_f32[...] + in_pl[...].astype(F32)).astype(BF16)
    folded = jnp.zeros((own, part_s), F32)
    for q in range(s_fold):
        folded = folded + dot(
            fold_pick(experts, rest, fold, q), c_rest[:, q * part_s : (q + 1) * part_s], ((1,), (0,))
        )
    c_left[...] = folded.astype(BF16)

    def start_back(p):
        for copy in back_copies(p, e):
            copy.start()

    each(experts, e, start_back)
    kept_back = [
        pltpu.make_async_copy(c_main.at[block(e)], r_main.at[block(e)], rc.at[e]),
        pltpu.make_async_copy(c_left.at[block(e)], r_left.at[block(e)], rcl.at[e]),
    ]
    for copy in kept_back:
        copy.start()

    @pl.loop(0, half // 512)
    def _(j):
        columns = pl.ds(pl.multiple_of(j * 512, 512), 512)
        grad_out[:, columns] = (
            dot(s_turn[...], x_main[:, columns], ((1,), (0,)))
            + dot(s_turn_rest[...], z[:, columns], ((1,), (0,)))
        ).astype(BF16)

    for copy in kept_back:
        copy.wait()

    def wait_back(s):
        for copy in back_copies(s, s):
            copy.wait_recv()

    each(experts, e, wait_back)
    ret_out[0:own, :] = r_main[...]
    for q in range(s_fold):
        ret_out[own : own + rest_own, q * part_s : (q + 1) * part_s] = dot(
            unfold_pick(experts, rest, fold, q), r_left[...], ((1,), (0,))
        ).astype(BF16)

    def drain_rows(p):
        for copy in row_copies(p, me):
            copy.wait_send()

    each(devices, me, drain_rows)

    def drain(p):
        for copy in scaled_copies(p, e) + back_copies(p, e):
            copy.wait_send()

    each(experts, e, drain)


def on_device(grad_out, saved_pre, gate_weight, routes, w_down):
    tokens, top_count = routes.shape
    hidden, half = w_down.shape[1:]
    width = grad_out.shape[1]
    experts = lax.axis_size("expert")
    replicas = lax.axis_size("dp")
    capacity = 5 * tokens * top_count // (4 * experts)
    if (replicas, top_count, capacity, hidden % 256, half % 512) != (2, 2, 20, 0, 0):
        return on_device_general(grad_out, saved_pre, gate_weight, routes, w_down)
    rest = capacity - BASE
    fold = BASE // rest
    s_fold = hidden // 256
    own, rest_own = experts * BASE, experts * rest
    devices = replicas * experts
    scaled = [
        scaled_hidden(saved_pre[:, k], gate_weight[:, k], hidden) for k in range(2)
    ]
    vmem = pl.BlockSpec(memory_space=pltpu.VMEM)
    *packed, positions = pl.pallas_call(
        functools.partial(pack_kernel, experts, rest, fold, replicas, s_fold),
        out_shape=(
            jax.ShapeDtypeStruct((own, width), BF16),
            jax.ShapeDtypeStruct((own, width // fold), BF16),
            jax.ShapeDtypeStruct((own, hidden), BF16),
            jax.ShapeDtypeStruct((own, 256), BF16),
            jax.ShapeDtypeStruct((2, tokens), jnp.int32),
        ),
        in_specs=[vmem] * 4,
        out_specs=[vmem] * 5,
    )(routes.T, grad_out, scaled[0], scaled[1])
    dma = pltpu.SemaphoreType.DMA
    total = devices * BASE
    back, grad_down = pl.pallas_call(
        functools.partial(exchange_kernel, experts, rest, fold, s_fold),
        out_shape=(
            jax.ShapeDtypeStruct((own + rest_own, hidden), BF16),
            jax.ShapeDtypeStruct((hidden, half), BF16),
        ),
        in_specs=[vmem] * 4 + [pl.BlockSpec(memory_space=pl.ANY)],
        out_specs=[vmem] * 2,
        scratch_shapes=[
            pltpu.VMEM((hidden, half), BF16),
            pltpu.VMEM((total, half), BF16),
            pltpu.VMEM((total, half // fold), BF16),
            pltpu.VMEM((devices * rest, half), BF16),
            pltpu.VMEM((total, hidden), BF16),
            pltpu.VMEM((total, 256), BF16),
            pltpu.VMEM((devices * rest, hidden), BF16),
            pltpu.VMEM((hidden, total), BF16),
            pltpu.VMEM((hidden, devices * rest), BF16),
            pltpu.VMEM((rest_own, hidden), F32),
            pltpu.VMEM((own, hidden), BF16),
            pltpu.VMEM((own, hidden), BF16),
            pltpu.VMEM((rest_own, hidden), BF16),
            pltpu.VMEM((rest_own, hidden), BF16),
            pltpu.VMEM((own, hidden), BF16),
            pltpu.VMEM((own, 256), BF16),
            pltpu.VMEM((own, hidden), BF16),
            pltpu.VMEM((own, 256), BF16),
            dma,
            dma((devices,)), dma((devices,)), dma((devices,)), dma((devices,)),
            dma((experts,)), dma((experts,)), dma((experts,)), dma((experts,)),
            dma((4,)), dma((4,)),
            dma((experts,)), dma((experts,)), dma((experts,)), dma((experts,)),
        ],
        compiler_params=pltpu.CompilerParams(collective_id=0, has_side_effects=True),
    )(*packed, w_down[0])
    slot_ids = jnp.arange(own + rest_own, dtype=jnp.int32)
    pick = (positions[:, :, None] == slot_ids).astype(BF16).reshape(2 * tokens, -1)
    contraction = dot(pick, back, ((1,), (0,))).astype(BF16).reshape(2, tokens, hidden)
    contraction = jnp.stack([contraction[0], contraction[1]], axis=1)
    grads, gate_grad = swiglu_grads(saved_pre, gate_weight, contraction, hidden)
    return grads, gate_grad, grad_down[None]


def solution(mesh):
    return jax.shard_map(
        on_device,
        mesh=mesh,
        in_specs=(
            P(("dp", "expert"), None),
            P(("dp", "expert"), None, None),
            P(("dp", "expert"), None),
            P(("dp", "expert"), None),
            P("expert", None, "dp"),
        ),
        out_specs=(
            P(("dp", "expert"), None, None),
            P(("dp", "expert"), None),
            P("expert", None, "dp"),
        ),
        check_vma=False,
    )
```

```python
import functools

import jax
import jax.numpy as jnp
from jax import lax
from jax.experimental import pallas as pl
from jax.experimental.pallas import tpu as pltpu
from jax.sharding import PartitionSpec as P

BF16 = jnp.bfloat16
F32 = jnp.float32


def slot_positions(routes_flat, experts, capacity):
    expert_ids = jnp.arange(experts, dtype=jnp.int32)
    onehot = (routes_flat[:, None] == expert_ids[None, :]).astype(jnp.int32)
    rank = jnp.sum((jnp.cumsum(onehot, axis=0) - 1) * onehot, axis=1)
    return routes_flat * capacity + rank


def swiglu_parts(saved, hidden):
    gate_pre = saved[..., :hidden].astype(F32)
    up_pre = saved[..., hidden:].astype(F32)
    return (gate_pre, up_pre, jax.nn.silu(gate_pre))


def swiglu_grads(saved, weights, contraction, hidden):
    gate_pre, up_pre, active = swiglu_parts(saved, hidden)
    plain = (active * up_pre).astype(BF16)
    gate_grad = jnp.sum(plain.astype(F32) * contraction.astype(F32), axis=-1).astype(BF16)
    back = weights.astype(F32)[..., None] * contraction.astype(F32)
    sigma = jax.nn.sigmoid(gate_pre)
    grad_gate_pre = back * up_pre * sigma * (1.0 + gate_pre * (1.0 - sigma))
    grad_up_pre = back * active
    return (jnp.concatenate([grad_gate_pre, grad_up_pre], axis=-1).astype(BF16), gate_grad)


def scaled_hidden(saved, weights, hidden):
    gate_pre, up_pre, active = swiglu_parts(saved, hidden)
    return (weights.astype(F32)[..., None] * active * up_pre).astype(BF16)


def dot(a, b, dims):
    return lax.dot_general(a, b, (dims, ((), ())), preferred_element_type=F32)


def on_device_general(grad_out, saved_pre, gate_weight, routes, w_down):
    tokens_dev, top_count = routes.shape
    hidden = w_down.shape[1]
    half = w_down.shape[2]
    experts = lax.axis_size("expert")
    replicas = lax.axis_size("dp")
    capacity = 5 * tokens_dev * top_count // (4 * experts)
    slots = experts * capacity
    positions = slot_positions(routes.reshape(-1), experts, capacity).reshape(tokens_dev, top_count)
    slot_ids = jnp.arange(slots, dtype=jnp.int32)
    picks = [
        (positions[:, k][None, :] == slot_ids[:, None]).astype(BF16) for k in range(top_count)
    ]
    pick = sum(picks[1:], picks[0])
    devices = replicas * experts
    send_rows = jnp.stack(
        [
            dot(pick, grad_out[:, d * half : (d + 1) * half], ((1,), (0,))).astype(BF16)
            for d in range(replicas)
        ]
    ).reshape(devices, capacity, half)
    scaled = scaled_hidden(saved_pre, gate_weight, hidden)
    send_scaled = sum(dot(picks[k], scaled[:, k], ((1,), (0,))) for k in range(top_count))
    send_scaled = send_scaled.astype(BF16).reshape(experts, capacity, hidden)
    rows = lax.all_to_all(send_rows, ("dp", "expert"), split_axis=0, concat_axis=0, tiled=True)
    scaled_in = lax.all_to_all(send_scaled, "expert", split_axis=0, concat_axis=0, tiled=True)
    scaled_in = lax.all_gather(scaled_in.reshape(slots, hidden), "dp", axis=0, tiled=True)
    rows = rows.reshape(devices * capacity, half)
    partial = dot(rows, w_down[0], ((1,), (1,))).astype(BF16).reshape(devices, capacity, hidden)
    parts = lax.all_to_all(partial, ("dp", "expert"), split_axis=0, concat_axis=0, tiled=True)
    parts = parts.reshape(replicas, slots, hidden)
    contraction = jnp.stack(
        [
            sum(dot(picks[k], parts[d], ((0,), (0,))) for d in range(replicas))
            for k in range(top_count)
        ],
        axis=1,
    ).astype(BF16)
    grads, gate_grad = swiglu_grads(saved_pre, gate_weight, contraction, hidden)
    grad_down = dot(scaled_in, rows, ((0,), (0,))).astype(BF16)
    return grads, gate_grad, grad_down[None]


BASE = 16
MESH = pl.DeviceIdType.MESH


def iota(shape, axis):
    return lax.broadcasted_iota(jnp.int32, shape, axis)


def unfold_pick(groups, rest, fold, q):
    shape = (groups * rest, groups * BASE)
    row, col = iota(shape, 0), iota(shape, 1)
    return (col == (row // rest) * BASE + q * rest + row % rest).astype(BF16)


def fold_pick(groups, rest, fold, q):
    shape = (groups * BASE, groups * rest)
    row, col = iota(shape, 0), iota(shape, 1)
    mine = (row // rest) % fold == q
    return (mine & (col == (row // BASE) * rest + row % rest)).astype(BF16)


def pack(
    experts, rest, fold, replicas, s_fold,
    routes, rows, scaled0, scaled1,
    main, left, smain, sleft, pos,
):
    tokens, width = rows.shape
    half = width // replicas
    part = half // fold
    count = experts * BASE
    names = iota((experts, tokens), 0)
    named = [(routes[k : k + 1, :] == names).astype(F32) for k in range(2)]
    before = (iota((tokens, tokens), 0) < iota((tokens, tokens), 1)).astype(BF16)
    counts = dot((named[0] + named[1]).astype(BF16), before, ((1,), (0,)))
    for k in range(2):
        rank = jnp.sum(counts * named[k], axis=0, keepdims=True).astype(jnp.int32)
        expert = routes[k : k + 1, :]
        pos[k : k + 1, :] = jnp.where(
            rank < BASE, expert * BASE + rank, count + expert * rest + rank - BASE
        )
    pos0, pos1 = pos[0:1, :], pos[1:2, :]
    row = iota((count, tokens), 0)
    pick0, pick1 = (pos0 == row).astype(BF16), (pos1 == row).astype(BF16)
    both = pick0 + pick1
    step = 1024
    for c in range(0, width, step):
        main[:, c : c + step] = dot(both, rows[:, c : c + step], ((1,), (0,))).astype(BF16)
    smain[...] = (
        dot(pick0, scaled0[...], ((1,), (0,))) + dot(pick1, scaled1[...], ((1,), (0,)))
    ).astype(BF16)
    slot = count + (row // BASE) * rest + row % rest
    total = [jnp.zeros((count, part), F32) for _ in range(replicas)]
    part_s = sleft.shape[1]
    total_s = jnp.zeros((count, part_s), F32)
    for q in range(fold):
        mine = (row // rest) % fold == q
        q0, q1 = ((pos0 == slot) & mine).astype(BF16), ((pos1 == slot) & mine).astype(BF16)
        for d in range(replicas):
            at = d * half + q * part
            total[d] = total[d] + dot(q0 + q1, rows[:, at : at + part], ((1,), (0,)))
        if q < s_fold:
            at = q * part_s
            total_s = total_s + dot(q0, scaled0[:, at : at + part_s], ((1,), (0,)))
            total_s = total_s + dot(q1, scaled1[:, at : at + part_s], ((1,), (0,)))
    for d in range(replicas):
        left[:, d * part : (d + 1) * part] = total[d].astype(BF16)
    sleft[...] = total_s.astype(BF16)


def exchange_kernel(
    experts, rest, fold, s_fold,
    routes, rows_in, scaled0, scaled1, w_hbm,
    ret_out, grad_out, pos,
    main, left, smain, sleft, w, x_main, x_left, z, s_main, s_left, s_rest, s_turn, s_turn_rest,
    mine_f32, out_px, in_px, out_pl, in_pl, c_main, c_left, r_main, r_left,
    w_sem, tx, rx, txl, rxl, ts, rs, tsl, rsl, tp, rp, tc, rc, tcl, rcl,
):
    d = lax.axis_index("dp")
    e = lax.axis_index("expert")
    other = 1 - d
    devices = 2 * experts
    me = d * experts + e
    half = w.shape[1]
    part = half // fold
    hidden = w.shape[0]
    part_s = sleft.shape[1]
    own, rest_own = experts * BASE, experts * rest

    def block(i):
        return pl.ds(pl.multiple_of(i * BASE, BASE), BASE)

    def remote(src, dst, send, recv, to):
        return pltpu.make_async_remote_copy(
            src_ref=src, dst_ref=dst, send_sem=send, recv_sem=recv, device_id=to, device_id_type=MESH
        )

    def row_copies(p, s):
        pd, pe = p // experts, p % experts
        wide = pl.ds(pl.multiple_of(pd * half, 128), half)
        narrow = pl.ds(pl.multiple_of(pd * part, 128), part)
        return (
            remote(main.at[block(pe), wide], x_main.at[block(s)], tx.at[p], rx.at[s], (pd, pe)),
            remote(left.at[block(pe), narrow], x_left.at[block(s)], txl.at[p], rxl.at[s], (pd, pe)),
        )

    def scaled_copies(pe, se):
        s = d * experts + se
        return (
            remote(smain.at[block(pe)], s_main.at[block(s)], ts.at[pe], rs.at[se], (d, pe)),
            remote(sleft.at[block(pe)], s_left.at[block(s)], tsl.at[pe], rsl.at[se], (d, pe)),
        )

    def back_copies(pe, se):
        return (
            remote(c_main.at[block(pe)], r_main.at[block(se)], tc.at[pe], rc.at[se], (d, pe)),
            remote(c_left.at[block(pe)], r_left.at[block(se)], tcl.at[pe], rcl.at[se], (d, pe)),
        )

    def each(count, position, body):
        def step(k, carry):
            body((position + 1 + (k + count // 2 - 1) % (count - 1)) % count)
            return carry

        lax.fori_loop(1, count, step, 0)

    fetch_w = pltpu.make_async_copy(w_hbm, w, w_sem)
    fetch_w.start()
    barrier = pltpu.get_barrier_semaphore()

    def greet(p):
        pl.semaphore_signal(
            barrier, inc=1, device_id=(p // experts, p % experts), device_id_type=MESH
        )

    each(devices, me, greet)
    pack(
        experts, rest, fold, 2, s_fold,
        routes, rows_in, scaled0, scaled1,
        main, left, smain, sleft, pos,
    )
    pl.semaphore_wait(barrier, devices - 1)

    def start_across(k, carry):
        for copy in row_copies(other * experts + (e + experts // 2 + k) % experts, me):
            copy.start()
        return carry

    lax.fori_loop(0, experts, start_across, 0)

    def start_scaled(p):
        for copy in scaled_copies(p, e):
            copy.start()

    each(experts, e, start_scaled)

    def start_rows(p):
        for copy in row_copies(d * experts + p, me):
            copy.start()

    each(experts, e, start_rows)
    kept = [
        pltpu.make_async_copy(
            main.at[block(e), pl.ds(pl.multiple_of(d * half, 128), half)], x_main.at[block(me)], rx.at[me]
        ),
        pltpu.make_async_copy(
            left.at[block(e), pl.ds(pl.multiple_of(d * part, 128), part)], x_left.at[block(me)], rxl.at[me]
        ),
        pltpu.make_async_copy(smain.at[block(e)], s_main.at[block(me)], rs.at[e]),
        pltpu.make_async_copy(sleft.at[block(e)], s_left.at[block(me)], rsl.at[e]),
    ]
    for copy in kept:
        copy.start()
    for copy in kept:
        copy.wait()
    fetch_w.wait()

    other_at, own_at = pl.multiple_of(other * own, own), pl.multiple_of(d * own, own)
    other_rest, own_rest = pl.multiple_of(other * rest_own, rest_own), pl.multiple_of(d * rest_own, rest_own)

    def unfold_rows(at, rest_at):
        for q in range(fold):
            z[pl.ds(rest_at, rest_own), q * part : (q + 1) * part] = dot(
                unfold_pick(experts, rest, fold, q), x_left[pl.ds(at, own), :], ((1,), (0,))
            ).astype(BF16)

    def contract(lo, ref, rows, start):
        return dot(ref[pl.ds(start, rows), :], w[lo : lo + 256, :], ((1,), (1,)))

    def wait_across(k, carry):
        s = other * experts + k
        for copy in row_copies(s, s):
            copy.wait_recv()
        return carry

    lax.fori_loop(0, experts, wait_across, 0)
    unfold_rows(other_at, other_rest)
    for lo in range(0, hidden, 256):
        out_px[:, lo : lo + 256] = contract(lo, x_main, own, other_at).astype(BF16)
        out_pl[:, lo : lo + 256] = contract(lo, z, rest_own, other_rest).astype(BF16)
    across = (other, e)
    px = remote(out_px, in_px, tp.at[0], rp.at[0], across)
    plx = remote(out_pl, in_pl, tp.at[1], rp.at[1], across)
    px.start()
    plx.start()

    def wait_scaled(s):
        for copy in scaled_copies(s, s):
            copy.wait_recv()

    each(experts, e, wait_scaled)
    region = pl.ds(own_at, own)
    forward = [
        remote(s_main.at[region], s_main.at[region], tp.at[2], rp.at[2], across),
        remote(s_left.at[region], s_left.at[region], tp.at[3], rp.at[3], across),
    ]
    for copy in forward:
        copy.start()
    px.wait()
    plx.wait()
    for copy in forward:
        copy.wait()
    for q in range(s_fold):
        s_rest[:, q * part_s : (q + 1) * part_s] = dot(
            unfold_pick(devices, rest, fold, q), s_left[...], ((1,), (0,))
        ).astype(BF16)
    s_turn[...] = s_main[...].T
    s_turn_rest[...] = s_rest[...].T

    def wait_rows(p):
        s = d * experts + p
        for copy in row_copies(s, s):
            copy.wait_recv()

    each(experts, e, wait_rows)
    unfold_rows(own_at, own_rest)
    for lo in range(0, hidden, 256):
        cut = slice(lo, lo + 256)
        c_main[:, cut] = (contract(lo, x_main, own, own_at) + in_px[:, cut].astype(F32)).astype(BF16)
        mine_f32[:, cut] = contract(lo, z, rest_own, own_rest)
    c_rest = (mine_f32[...] + in_pl[...].astype(F32)).astype(BF16)
    folded = jnp.zeros((own, part_s), F32)
    for q in range(s_fold):
        folded = folded + dot(
            fold_pick(experts, rest, fold, q), c_rest[:, q * part_s : (q + 1) * part_s], ((1,), (0,))
        )
    c_left[...] = folded.astype(BF16)

    def start_back(p):
        for copy in back_copies(p, e):
            copy.start()

    each(experts, e, start_back)
    kept_back = [
        pltpu.make_async_copy(c_main.at[block(e)], r_main.at[block(e)], rc.at[e]),
        pltpu.make_async_copy(c_left.at[block(e)], r_left.at[block(e)], rcl.at[e]),
    ]
    for copy in kept_back:
        copy.start()

    @pl.loop(0, half // 512)
    def _(j):
        columns = pl.ds(pl.multiple_of(j * 512, 512), 512)
        grad_out[:, columns] = (
            dot(s_turn[...], x_main[:, columns], ((1,), (0,)))
            + dot(s_turn_rest[...], z[:, columns], ((1,), (0,)))
        ).astype(BF16)

    for copy in kept_back:
        copy.wait()

    def wait_back(s):
        for copy in back_copies(s, s):
            copy.wait_recv()

    each(experts, e, wait_back)
    ret_out[0:own, :] = r_main[...]
    for q in range(s_fold):
        ret_out[own : own + rest_own, q * part_s : (q + 1) * part_s] = dot(
            unfold_pick(experts, rest, fold, q), r_left[...], ((1,), (0,))
        ).astype(BF16)

    def drain_rows(p):
        for copy in row_copies(p, me):
            copy.wait_send()

    each(devices, me, drain_rows)

    def drain(p):
        for copy in scaled_copies(p, e) + back_copies(p, e):
            copy.wait_send()

    each(experts, e, drain)


def on_device(grad_out, saved_pre, gate_weight, routes, w_down):
    tokens, top_count = routes.shape
    hidden, half = w_down.shape[1:]
    width = grad_out.shape[1]
    experts = lax.axis_size("expert")
    replicas = lax.axis_size("dp")
    capacity = 5 * tokens * top_count // (4 * experts)
    if (replicas, top_count, capacity, hidden % 256, half % 512) != (2, 2, 20, 0, 0):
        return on_device_general(grad_out, saved_pre, gate_weight, routes, w_down)
    rest = capacity - BASE
    fold = BASE // rest
    s_fold = hidden // 256
    own, rest_own = experts * BASE, experts * rest
    devices = replicas * experts
    scaled = [
        scaled_hidden(saved_pre[:, k], gate_weight[:, k], hidden) for k in range(2)
    ]
    vmem = pl.BlockSpec(memory_space=pltpu.VMEM)
    dma = pltpu.SemaphoreType.DMA
    total = devices * BASE
    back, grad_down, positions = pl.pallas_call(
        functools.partial(exchange_kernel, experts, rest, fold, s_fold),
        out_shape=(
            jax.ShapeDtypeStruct((own + rest_own, hidden), BF16),
            jax.ShapeDtypeStruct((hidden, half), BF16),
            jax.ShapeDtypeStruct((2, tokens), jnp.int32),
        ),
        in_specs=[vmem] * 4 + [pl.BlockSpec(memory_space=pl.ANY)],
        out_specs=[vmem] * 3,
        scratch_shapes=[
            pltpu.VMEM((own, width), BF16),
            pltpu.VMEM((own, width // fold), BF16),
            pltpu.VMEM((own, hidden), BF16),
            pltpu.VMEM((own, 256), BF16),
            pltpu.VMEM((hidden, half), BF16),
            pltpu.VMEM((total, half), BF16),
            pltpu.VMEM((total, half // fold), BF16),
            pltpu.VMEM((devices * rest, half), BF16),
            pltpu.VMEM((total, hidden), BF16),
            pltpu.VMEM((total, 256), BF16),
            pltpu.VMEM((devices * rest, hidden), BF16),
            pltpu.VMEM((hidden, total), BF16),
            pltpu.VMEM((hidden, devices * rest), BF16),
            pltpu.VMEM((rest_own, hidden), F32),
            pltpu.VMEM((own, hidden), BF16),
            pltpu.VMEM((own, hidden), BF16),
            pltpu.VMEM((rest_own, hidden), BF16),
            pltpu.VMEM((rest_own, hidden), BF16),
            pltpu.VMEM((own, hidden), BF16),
            pltpu.VMEM((own, 256), BF16),
            pltpu.VMEM((own, hidden), BF16),
            pltpu.VMEM((own, 256), BF16),
            dma,
            dma((devices,)), dma((devices,)), dma((devices,)), dma((devices,)),
            dma((experts,)), dma((experts,)), dma((experts,)), dma((experts,)),
            dma((4,)), dma((4,)),
            dma((experts,)), dma((experts,)), dma((experts,)), dma((experts,)),
        ],
        compiler_params=pltpu.CompilerParams(collective_id=0, has_side_effects=True),
    )(routes.T, grad_out, scaled[0], scaled[1], w_down[0])
    slot_ids = jnp.arange(own + rest_own, dtype=jnp.int32)
    pick = (positions[:, :, None] == slot_ids).astype(BF16).reshape(2 * tokens, -1)
    contraction = dot(pick, back, ((1,), (0,))).astype(BF16).reshape(2, tokens, hidden)
    contraction = jnp.stack([contraction[0], contraction[1]], axis=1)
    grads, gate_grad = swiglu_grads(saved_pre, gate_weight, contraction, hidden)
    return grads, gate_grad, grad_down[None]


def solution(mesh):
    return jax.shard_map(
        on_device,
        mesh=mesh,
        in_specs=(
            P(("dp", "expert"), None),
            P(("dp", "expert"), None, None),
            P(("dp", "expert"), None),
            P(("dp", "expert"), None),
            P("expert", None, "dp"),
        ),
        out_specs=(
            P(("dp", "expert"), None, None),
            P(("dp", "expert"), None),
            P("expert", None, "dp"),
        ),
        check_vma=False,
    )
```
